32 devices in a mesh: mp: 2 (over core), gx: 2 (over y), gy: 8 (over z, x).
Axes of the slice: x: 2, y: 2, z: 4, core: 2. Of those that a mesh axis runs over, the one named last changes fastest.
Arguments:
- action: bfloat16 [8, 24, 64, 1024], P(None, None, ('mp', 'gx'), 'gy'), may hold values from 0.049804688 to 2
- land_mask: int32 [64, 1024], P(('mp', 'gx'), 'gy'), may hold values 0 or 1
- bathymetry: float32 [64, 1024], P(('mp', 'gx', 'gy')), may hold values from 8 to 40
- surge: float32 [64, 1024], P(('mp', 'gx', 'gy')), may hold values from -3 to 3
- ocean_fields: float32 [4, 16, 64, 1024], P(None, None, ('mp', 'gx', 'gy')), may hold values from -2.5 to 2.5
- layer_share: float32 [16], replicated, may hold values from 0.5 to 2
Outputs:
- new_action: bfloat16 [8, 24, 64, 1024], P(None, None, ('mp', 'gx'), 'gy')
- new_fields: float32 [4, 16, 64, 1024], P(None, None, ('mp', 'gx', 'gy'))
The draws below stay inside these ranges and needn't reach their ends.
All inputs are finite; a program needn't handle non-finite values. No bound on the sum of `land_mask` on one device may be relied on, other than what follows from the above.
Results may differ from the reference program's by a relative error of at most 0.0046.
Values may be sent and summed in bfloat16 or wider, within the bound.
A program may use at most 64 MiB of HBM per device.

```python
import math
import jax
import jax.numpy as jnp
from jax import lax

FREQ = 8
DIRS = 24
LEV = 16
FIELDS = 4
STEPS = 4
NY = 64
NX = 1024


def touch_ends(drawn, own_key, low, high):
    shape = drawn.shape
    spot = [jax.random.randint(jax.random.fold_in(own_key, axis), (), 0, shape[axis]) for axis in range(len(shape))]
    drawn = drawn.at[tuple(spot)].set(low)
    longest = shape.index(max(shape))
    spot[longest] = (spot[longest] + 1) % shape[longest]
    return drawn.at[tuple(spot)].set(high)


def block_levels(key, extent, shards, low, top_value):
    def one(dim, parts):
        draws = jax.random.uniform(jax.random.fold_in(jax.random.fold_in(key, 6), dim), (parts,), jnp.float32, low / len(shards), top_value / len(shards))
        return jnp.repeat(jnp.exp(draws), extent[dim] // parts).reshape((-1,) + (1,) * (len(extent) - dim - 1))

    factor_of = one(*shards[0])
    for cut in shards[1:]:
        factor_of = factor_of * one(*cut)
    return factor_of


def scatter_about(stream_key, extent, scale, limit, split=(), kind=jnp.bfloat16):
    gain = block_levels(stream_key, extent, split, -0.22, 0.18) if split else 1.0
    result = jax.random.normal(stream_key, extent, jnp.float32) * scale * gain
    return jnp.minimum(jnp.maximum(result, -limit), limit).astype(kind)


def setup_inputs(seed: int = 0) -> dict:
    splits = jax.random.split(jax.random.key(seed), 7)
    return {
        "action": jnp.clip(jnp.exp(math.log(2.0) - 3.6927934 * jax.random.uniform(splits[0], (FREQ, DIRS, NY, NX), jnp.float32) ** block_levels(splits[0], (FREQ, DIRS, NY, NX), ((2, 4), (3, 8)), -0.2, 0.2)), 0.049804688, 2.0).astype(jnp.bfloat16),
        "land_mask": touch_ends((jax.random.randint(splits[1], (NY, NX), 0, 8) < 7).astype(jnp.int32), jax.random.fold_in(splits[1], 1), 0, 1),
        "bathymetry": jnp.clip(jnp.exp(math.log(40.0) - 1.609438 * jax.random.uniform(splits[2], (NY, NX), jnp.float32) ** block_levels(splits[2], (NY, NX), ((0, 32),), -0.2, 0.2)), 8.0, 40.0),
        "surge": jnp.clip(jax.random.uniform(splits[3], (NY, NX), jnp.float32, -3.0, 3.0) * block_levels(splits[3], (NY, NX), ((0, 32),), -0.4, 0.0), -3.0, 3.0),
        "ocean_fields": scatter_about(splits[4], (FIELDS, LEV, NY, NX), 1.0, 2.5, ((2, 32),), jnp.float32),
        "layer_share": jnp.clip(jnp.exp(jax.random.uniform(splits[5], (LEV,), jnp.float32, math.log(0.5), math.log(2.0))), 0.5, 2.0),
    }


GRAVITY = 9.81
STEP_TIME = 14.0
CELL_SIZE = 500.0
FIRST_FREQ = 0.05
FREQ_RATIO = 1.1
MIXING = 0.2
PUSH_SCALE = 20.0

def spectral_tables(band_count, direction_count):
    radian = 2.0 * math.pi * FIRST_FREQ * jnp.power(FREQ_RATIO, jnp.arange(band_count).astype(jnp.float32))
    angles = jnp.arange(direction_count).astype(jnp.float32) * (2.0 * math.pi / direction_count)
    return (radian, jnp.cos(angles), jnp.sin(angles))

def wave_coefficients(radian_freq, water_depth):
    angular = radian_freq[:, None, None]
    deep_number = angular * angular / GRAVITY
    wave_number = deep_number / jnp.sqrt(jnp.tanh(deep_number * water_depth[None]))
    twice_kh = 2.0 * wave_number * water_depth[None]
    shoal_ratio = 0.5 * (1.0 + twice_kh / jnp.sinh(twice_kh))
    group_speed = shoal_ratio * angular / wave_number
    bend_factor = angular / jnp.sinh(twice_kh)
    return (shoal_ratio, group_speed, bend_factor)

def velocities(group_speed, bend_factor, cosine_table, sine_table, mean_east, mean_north, slope_east, slope_north):
    cos_dir = cosine_table[None, :, None, None]
    sin_dir = sine_table[None, :, None, None]
    courant = STEP_TIME / CELL_SIZE
    turn_scale = STEP_TIME / (2.0 * CELL_SIZE * (2.0 * math.pi / cosine_table.shape[0]))
    step_east = courant * (group_speed[:, None] * cos_dir + mean_east[None, None])
    step_north = courant * (group_speed[:, None] * sin_dir + mean_north[None, None])
    raw_turn = turn_scale * bend_factor[:, None] * (sin_dir * slope_east[None, None] - cos_dir * slope_north[None, None])
    return (step_east, step_north, raw_turn / (1.0 + jnp.abs(raw_turn)))

def advance(padded, step_east, step_north, turn_rate, wet_cells):
    center = padded[:, :, 1:-1, 1:-1].astype(jnp.float32)
    west_side = padded[:, :, 1:-1, :-2].astype(jnp.float32)
    east_side = padded[:, :, 1:-1, 2:].astype(jnp.float32)
    south_side = padded[:, :, :-2, 1:-1].astype(jnp.float32)
    north_side = padded[:, :, 2:, 1:-1].astype(jnp.float32)
    advected = center - jnp.maximum(step_east, 0.0) * (center - west_side) - jnp.minimum(step_east, 0.0) * (east_side - center) - jnp.maximum(step_north, 0.0) * (center - south_side) - jnp.minimum(step_north, 0.0) * (north_side - center)
    before = jnp.roll(advected, 1, axis=1)
    following = jnp.roll(advected, -1, axis=1)
    turned = advected - jnp.maximum(turn_rate, 0.0) * (advected - before) - jnp.minimum(turn_rate, 0.0) * (following - advected)
    return (wet_cells[None, None] * turned).astype(jnp.bfloat16)

def stresses(spectrum, radian_freq, shoal_ratio, cosine_table, sine_table):
    energy = radian_freq[:, None, None, None] * spectrum.astype(jnp.float32)
    ratio = shoal_ratio[:, None]
    cos_sq = (cosine_table * cosine_table)[None, :, None, None]
    sin_sq = (sine_table * sine_table)[None, :, None, None]
    cross = (cosine_table * sine_table)[None, :, None, None]
    stress_xx = lax.optimization_barrier(jnp.sum(energy * (ratio * (cos_sq + 1.0) - 0.5), axis=(0, 1)))
    stress_xy = lax.optimization_barrier(jnp.sum(energy * ratio * cross, axis=(0, 1)))
    stress_yy = lax.optimization_barrier(jnp.sum(energy * (ratio * (sin_sq + 1.0) - 0.5), axis=(0, 1)))
    return jnp.stack([stress_xx, stress_xy, stress_yy])

def divergence(padded_stress, water_depth):
    east_diff = padded_stress[:, 1:-1, 2:] - padded_stress[:, 1:-1, :-2]
    north_diff = padded_stress[:, 2:, 1:-1] - padded_stress[:, :-2, 1:-1]
    force_east = -(east_diff[0] + north_diff[1]) / (2.0 * water_depth)
    force_north = -(east_diff[1] + north_diff[2]) / (2.0 * water_depth)
    return jnp.stack([force_east, force_north])

def vertical_mix(fields):
    upper = jnp.concatenate([fields[:, :1], fields[:, :-1]], axis=1)
    lower = jnp.concatenate([fields[:, 1:], fields[:, -1:]], axis=1)
    return fields + MIXING * (upper - 2.0 * fields + lower)

def apply_push(fields, forces, layer_weight):
    mixed = vertical_mix(fields)
    spare = jnp.zeros((fields.shape[0] - 2,) + forces.shape[1:], jnp.float32)
    forcing = jnp.concatenate([forces, spare], axis=0)
    return mixed + PUSH_SCALE * fields.shape[1] * layer_weight[None, :, None, None] * forcing[:, None]

def reference(action, land_mask, bathymetry, surge, ocean_fields, layer_share):
    water_depth = bathymetry + surge
    layer_weight = layer_share / jnp.sum(layer_share)
    mean_east = lax.optimization_barrier(jnp.sum(layer_weight[:, None, None] * ocean_fields[0], axis=0))
    mean_north = lax.optimization_barrier(jnp.sum(layer_weight[:, None, None] * ocean_fields[1], axis=0))
    row_ids = jnp.arange(NY)[:, None]
    col_ids = jnp.arange(NX)[None, :]
    inner_cells = ((row_ids > 0) & (row_ids < NY - 1) & (col_ids > 0) & (col_ids < NX - 1)).astype(jnp.float32)
    wet_cells = land_mask.astype(jnp.float32) * inner_cells
    padded_depth = jnp.pad(water_depth, 1)
    slope_east = padded_depth[1:-1, 2:] - padded_depth[1:-1, :-2]
    slope_north = padded_depth[2:, 1:-1] - padded_depth[:-2, 1:-1]
    radian_freq, cosine_table, sine_table = spectral_tables(FREQ, DIRS)

    def one_band(inputs):
        band_action, band_radian = inputs
        single = band_radian[None]
        shoal_ratio, group_speed, bend_factor = wave_coefficients(single, water_depth)
        step_east, step_north, turn_rate = velocities(group_speed, bend_factor, cosine_table, sine_table, mean_east, mean_north, slope_east, slope_north)
        spectrum = band_action[None]
        for step_index in range(STEPS):
            padded = jnp.pad(spectrum, ((0, 0), (0, 0), (1, 1), (1, 1)))
            spectrum = advance(padded, step_east, step_north, turn_rate, wet_cells)
        return (spectrum[0], stresses(spectrum, single, shoal_ratio, cosine_table, sine_table))
    new_action, band_stress = lax.map(one_band, (action, radian_freq))
    stress_field = lax.optimization_barrier(jnp.sum(band_stress, axis=0)) / (FREQ * DIRS)
    forces = divergence(jnp.pad(stress_field, ((0, 0), (1, 1), (1, 1))), water_depth)
    new_fields = apply_push(ocean_fields, forces, layer_weight)
    return (new_action, new_fields)
```

```python
import functools
import math

import jax
import jax.numpy as jnp
import numpy as np
from jax import lax
from jax.experimental import pallas as pl
from jax.experimental.pallas import tpu as pltpu
from jax.sharding import PartitionSpec as P

STEPS = 4
GRAVITY = 9.81
STEP_TIME = 14.0
CELL_SIZE = 500.0
FIRST_FREQ = 0.05
FREQ_RATIO = 1.1
MIXING = 0.2
PUSH_SCALE = 20.0
LANES = 128
TOP = 8
MESH = pl.DeviceIdType.MESH


def kernel(
    mesh_mp,
    mesh_gx,
    n,
    action_ref,
    land_ref,
    bath_ref,
    surge_ref,
    ocean_ref,
    share_ref,
    out_ref,
    fields_ref,
    pk,
    rx,
    tile,
    dpad,
    dhalo,
    ccg,
    sn,
    hs,
    tb,
    qs,
    xs,
    ps,
    ew_send,
    ew_recv,
    ns_send,
    ns_recv,
    st,
    spad,
    shalo,
    pk2,
    rx2,
    a2a_send,
    a2a_recv,
    back_send,
    back_recv,
    dep_send,
    dep_recv,
    str_send,
    str_recv,
    ew_ssem,
    ew_rsem,
    ns_ssem,
    ns_rsem,
):
    freqs, dirs, rows, cols = action_ref.shape
    levels, strip = ocean_ref.shape[1], ocean_ref.shape[2]
    wide = ocean_ref.shape[3]
    row_count = mesh_mp * mesh_gx
    mp, gx, me = lax.axis_index("mp"), lax.axis_index("gx"), lax.axis_index("gy")
    rank = mp * mesh_gx + gx
    has_south, has_north = rank > 0, rank < row_count - 1
    has_west, has_east = me > 0, me < n - 1
    south_rank = lax.rem(rank + row_count - 1, row_count)
    north_rank = lax.rem(rank + 1, row_count)
    south = (lax.div(south_rank, mesh_gx), lax.rem(south_rank, mesh_gx), me)
    north = (lax.div(north_rank, mesh_gx), lax.rem(north_rank, mesh_gx), me)
    west = (mp, gx, lax.rem(me + n - 1, n))
    east = (mp, gx, lax.rem(me + 1, n))
    angles = np.arange(dirs) * (2.0 * math.pi / dirs)
    cosine = [float(np.float32(v)) for v in np.cos(angles)]
    sine = [float(np.float32(v)) for v in np.sin(angles)]
    courant = STEP_TIME / CELL_SIZE
    turn_scale = STEP_TIME / (2.0 * CELL_SIZE * (2.0 * math.pi / dirs))

    barrier = pltpu.get_barrier_semaphore()
    for off in range(1, n):
        pl.semaphore_signal(
            barrier, inc=1, device_id=(mp, gx, lax.rem(me + off, n)), device_id_type=MESH
        )

    @pl.when(has_south)
    def _():
        pl.semaphore_signal(barrier, inc=1, device_id=south, device_id_type=MESH)

    @pl.when(has_north)
    def _():
        pl.semaphore_signal(barrier, inc=1, device_id=north, device_id_type=MESH)

    total = share_ref[0]
    for level in range(1, levels):
        total = total + share_ref[level]
    total_row = jnp.full((strip, wide), total, jnp.float32)
    for field in range(2):
        mean = share_ref[0] * ocean_ref[field, 0]
        for level in range(1, levels):
            mean = mean + share_ref[level] * ocean_ref[field, level]
        pk[field * strip : (field + 1) * strip, :] = mean / total_row
    pk[2 * strip : 3 * strip, :] = bath_ref[...] + surge_ref[...]
    wide_lane = lax.broadcasted_iota(jnp.int32, (8, wide), 1)

    def east_diff(value):
        after = jnp.where(wide_lane == wide - 1, 0.0, pltpu.roll(value, wide - 1, 1))
        before = jnp.where(wide_lane == 0, 0.0, pltpu.roll(value, 1, 1))
        return after - before

    pk[8:16, :] = east_diff(pk[0:8, :])
    pk[3 * strip : 4 * strip, :] = pk[8 + 2 * strip : 8 + 3 * strip, :]

    pl.semaphore_wait(barrier, n - 1 + has_south.astype(jnp.int32) + has_north.astype(jnp.int32))

    def strip_copy(off):
        peer = lax.rem(me + off, n)
        return pltpu.make_async_remote_copy(
            src_ref=pk.at[0:8, pl.ds(pl.multiple_of(peer * LANES, LANES), LANES)],
            dst_ref=rx.at[me],
            send_sem=a2a_send.at[off],
            recv_sem=a2a_recv.at[off],
            device_id=(mp, gx, peer),
            device_id_type=MESH,
        )

    for off in range(1, n):
        strip_copy(off).start()
    rx[me] = pk[0:8, pl.ds(pl.multiple_of(me * LANES, LANES), LANES)]

    def ew_copy(step, freq, side):
        return pltpu.make_async_remote_copy(
            src_ref=ew_send.at[step, freq],
            dst_ref=ew_recv.at[side, step, freq],
            send_sem=ew_ssem.at[side, step, freq],
            recv_sem=ew_rsem.at[side, step, freq],
            device_id=east if side == 0 else west,
            device_id_type=MESH,
        )

    def ns_copy(step, freq, side):
        return pltpu.make_async_remote_copy(
            src_ref=ns_send.at[side, step, freq],
            dst_ref=ns_recv.at[side, step, freq],
            send_sem=ns_ssem.at[side, step, freq],
            recv_sem=ns_rsem.at[side, step, freq],
            device_id=north if side == 0 else south,
            device_id_type=MESH,
        )

    def send_edges(step, freq):
        @pl.when(has_east)
        def _():
            ew_copy(step, freq, 0).start()

        @pl.when(has_west)
        def _():
            ew_copy(step, freq, 1).start()

        @pl.when(has_north)
        def _():
            ns_copy(step, freq, 0).start()

        @pl.when(has_south)
        def _():
            ns_copy(step, freq, 1).start()

    def recv_edges(step, freq):
        @pl.when(has_west)
        def _():
            ew_copy(step, freq, 0).wait_recv()

        @pl.when(has_east)
        def _():
            ew_copy(step, freq, 1).wait_recv()

        @pl.when(has_south)
        def _():
            ns_copy(step, freq, 0).wait_recv()

        @pl.when(has_north)
        def _():
            ns_copy(step, freq, 1).wait_recv()

    def drain_edges(step, freq):
        @pl.when(has_east)
        def _():
            ew_copy(step, freq, 0).wait_send()

        @pl.when(has_west)
        def _():
            ew_copy(step, freq, 1).wait_send()

        @pl.when(has_north)
        def _():
            ns_copy(step, freq, 0).wait_send()

        @pl.when(has_south)
        def _():
            ns_copy(step, freq, 1).wait_send()

    @pl.when(jnp.logical_not(has_west))
    def _():
        ew_recv[0] = jnp.zeros(ew_recv.shape[1:], jnp.float32)

    @pl.when(jnp.logical_not(has_east))
    def _():
        ew_recv[1] = jnp.zeros(ew_recv.shape[1:], jnp.float32)

    @pl.when(jnp.logical_not(has_south))
    def _():
        ns_recv[0] = jnp.zeros(ns_recv.shape[1:], jnp.float32)
        dhalo[0] = jnp.zeros(dhalo.shape[1:], jnp.float32)
        shalo[0] = jnp.zeros(shalo.shape[1:], jnp.float32)

    @pl.when(jnp.logical_not(has_north))
    def _():
        ns_recv[1] = jnp.zeros(ns_recv.shape[1:], jnp.float32)
        dhalo[1] = jnp.zeros(dhalo.shape[1:], jnp.float32)
        shalo[1] = jnp.zeros(shalo.shape[1:], jnp.float32)

    lane = lax.broadcasted_iota(jnp.int32, (rows, cols), 1)
    pair = lane // 2
    even = lane % 2 == 0
    first_lane, last_lane = lane == 0, lane == cols - 1

    def keep(step, freq, d, value, packed):
        xs[freq, d, TOP : TOP + rows, :] = value
        ns_send[0, step, freq, d : d + 1, :] = value[rows - 1 : rows, :]
        ns_send[1, step, freq, d : d + 1, :] = value[0:1, :]
        turned = pltpu.roll(value, 2 * d + 1, 1)
        return jnp.where(pair == d, turned, packed)

    def first_edges(freq, carry):
        packed = jnp.zeros((rows, cols), jnp.float32)
        for d in range(dirs):
            packed = keep(0, freq, d, action_ref[freq, d].astype(jnp.float32), packed)
        ew_send[0, freq] = packed
        send_edges(0, freq)
        return carry

    lax.fori_loop(0, freqs, first_edges, 0)

    for field in range(ocean_ref.shape[0]):
        for level in range(levels):
            here = ocean_ref[field, level]
            upper = ocean_ref[field, max(level - 1, 0)]
            lower = ocean_ref[field, min(level + 1, levels - 1)]
            fields_ref[field, level] = here + MIXING * (upper - 2.0 * here + lower)

    for off in range(1, n):
        strip_copy(off).wait_recv()
    for g in range(n):
        for item in range(4):
            tile[item, g * strip : (g + 1) * strip, :] = rx[g, item * strip : (item + 1) * strip, :]

    def depth_copy(side):
        return pltpu.make_async_remote_copy(
            src_ref=tile.at[2, rows - 8 : rows] if side == 0 else tile.at[2, 0:8],
            dst_ref=dhalo.at[side],
            send_sem=dep_send.at[side],
            recv_sem=dep_recv.at[side],
            device_id=north if side == 0 else south,
            device_id_type=MESH,
        )

    def stress_copy(side):
        return pltpu.make_async_remote_copy(
            src_ref=st.at[1:3, rows - 8 : rows] if side == 0 else st.at[1:3, 0:8],
            dst_ref=shalo.at[side],
            send_sem=str_send.at[side],
            recv_sem=str_recv.at[side],
            device_id=north if side == 0 else south,
            device_id_type=MESH,
        )

    def start_pair(copy):
        @pl.when(has_north)
        def _():
            copy(0).start()

        @pl.when(has_south)
        def _():
            copy(1).start()

    def wait_pair(copy):
        @pl.when(has_south)
        def _():
            copy(0).wait_recv()

        @pl.when(has_north)
        def _():
            copy(1).wait_recv()

    def drain_pair(copy):
        @pl.when(has_north)
        def _():
            copy(0).wait_send()

        @pl.when(has_south)
        def _():
            copy(1).wait_send()

    start_pair(depth_copy)
    depth = tile[2]
    share_of = 1.0 / (freqs * dirs)
    for f in range(freqs):
        sigma = 2.0 * math.pi * FIRST_FREQ * FREQ_RATIO**f
        deep = sigma * sigma / GRAVITY
        number = deep / jnp.sqrt(jnp.tanh(deep * depth))
        twice = 2.0 * number * depth
        grown = jnp.exp(twice)
        inv_sinh = 2.0 / (grown - 1.0 / grown)
        ratio = 0.5 * (1.0 + twice * inv_sinh)
        ccg[f] = (courant * sigma) * ratio / number
        tb[f] = (turn_scale * sigma) * inv_sinh
        sn[f] = (sigma * share_of) * ratio
        hs[f] = jnp.full((rows, cols), 0.5 * sigma * share_of, jnp.float32)
    dpad[TOP : TOP + rows, :] = depth
    wait_pair(depth_copy)
    dpad[TOP - 1 : TOP, :] = dhalo[0, 7:8, :]
    dpad[TOP + rows : TOP + rows + 1, :] = dhalo[1, 0:1, :]
    slope_north = dpad[TOP + 1 : TOP + 1 + rows, :] - dpad[TOP - 1 : TOP - 1 + rows, :]
    slope_east = tile[3]
    for d in range(dirs // 2):
        ps[d] = sine[d] * slope_east - cosine[d] * slope_north

    def turn_rates(freq, carry):
        scale = tb[freq]
        for d in range(dirs // 2):
            raw = scale * ps[d]
            qs[freq, d] = raw / (1.0 + jnp.abs(raw))
        return carry

    lax.fori_loop(0, freqs, turn_rates, 0)
    row = lax.broadcasted_iota(jnp.int32, (rows, cols), 0) + rank * rows
    col = lane + me * cols
    inner = (row > 0) & (row < row_count * rows - 1) & (col > 0) & (col < wide - 1)
    tile[3] = jnp.where(inner, land_ref[...].astype(jnp.float32), 0.0)
    tile[0] = courant * tile[0]
    tile[1] = courant * tile[1]

    def advance(index, carry):
        step, freq = lax.div(index, freqs), lax.rem(index, freqs)
        recv_edges(step, freq)
        merged = jnp.where(
            even,
            pltpu.roll(ew_recv[1, step, freq], cols - 1, 1),
            pltpu.roll(ew_recv[0, step, freq], 1, 1),
        )
        speed = ccg[freq]
        mean_east, mean_north = tile[0], tile[1]
        for d in range(dirs):
            xs[freq, d, TOP - 1 : TOP, :] = ns_recv[0, step, freq, d : d + 1, :]
            xs[freq, d, TOP + rows : TOP + rows + 1, :] = ns_recv[1, step, freq, d : d + 1, :]
        for d in range(dirs):
            value = xs[freq, d, TOP : TOP + rows, :]
            below = xs[freq, d, TOP - 1 : TOP - 1 + rows, :]
            above = xs[freq, d, TOP + 1 : TOP + 1 + rows, :]
            edge = pltpu.roll(merged, cols - 2 * d - 1, 1)
            left = jnp.where(first_lane, edge, pltpu.roll(value, 1, 1))
            right = jnp.where(last_lane, edge, pltpu.roll(value, cols - 1, 1))
            ax = speed * cosine[d] + mean_east
            ay = speed * sine[d] + mean_north
            ps[d] = (
                value
                - jnp.abs(ax) * (value - jnp.where(ax > 0.0, left, right))
                - jnp.abs(ay) * (value - jnp.where(ay > 0.0, below, above))
            )
        wet = tile[3]
        after = lax.rem(step + 1, STEPS)
        packed = jnp.zeros((rows, cols), jnp.float32)
        for d in range(dirs):
            half = d % (dirs // 2)
            rate = qs[freq, half]
            value = ps[d]
            before, following = ps[(d - 1) % dirs], ps[(d + 1) % dirs]
            if d >= dirs // 2:
                before, following = following, before
            turned = value - jnp.abs(rate) * (value - jnp.where(rate > 0.0, before, following))
            rounded = (wet * turned).astype(jnp.bfloat16)
            out_ref[freq, d] = rounded
            value = rounded.astype(jnp.float32)
            xs[freq, d, TOP : TOP + rows, :] = value
            packed = jnp.where(pair == d, pltpu.roll(value, 2 * d + 1, 1), packed)

        @pl.when(step < STEPS - 1)
        def _():
            ew_send[after, freq] = packed
            for d in range(dirs):
                ns_send[0, after, freq, d : d + 1, :] = xs[
                    freq, d, TOP + rows - 1 : TOP + rows, :
                ]
                ns_send[1, after, freq, d : d + 1, :] = xs[freq, d, TOP : TOP + 1, :]
            send_edges(after, freq)

        return carry

    lax.fori_loop(0, STEPS * freqs, advance, 0)

    def stress(freq, carry):
        plain = jnp.zeros((rows, cols), jnp.float32)
        cos_sq, cross = plain, plain
        for d in range(dirs):
            value = xs[freq, d, TOP : TOP + rows, :]
            plain = plain + value
            cos_sq = cos_sq + (cosine[d] * cosine[d]) * value
            cross = cross + (cosine[d] * sine[d]) * value
        scaled, half = sn[freq], hs[freq] * plain
        return (
            carry[0] + scaled * (cos_sq + plain) - half,
            carry[1] + scaled * cross,
            carry[2] + scaled * (2.0 * plain - cos_sq) - half,
        )

    zero = jnp.zeros((rows, cols), jnp.float32)
    sums = lax.fori_loop(0, freqs, stress, (zero, zero, zero))
    for item in range(3):
        st[item] = sums[item]
    start_pair(stress_copy)
    for item in range(2):
        spad[item, TOP : TOP + rows, :] = sums[1 + item]
    wait_pair(stress_copy)
    for item in range(2):
        spad[item, TOP - 1 : TOP, :] = shalo[0, item, 7:8, :]
        spad[item, TOP + rows : TOP + rows + 1, :] = shalo[1, item, 0:1, :]
    for item in range(2):
        tile[item] = (
            spad[item, TOP + 1 : TOP + 1 + rows, :] - spad[item, TOP - 1 : TOP - 1 + rows, :]
        )
    for g in range(n):
        span = slice(g * strip, (g + 1) * strip)
        pk2[g, 0:strip, :] = st[0, span, :]
        pk2[g, strip : 2 * strip, :] = st[1, span, :]
        pk2[g, 2 * strip : 3 * strip, :] = tile[0, span, :]
        pk2[g, 3 * strip : 4 * strip, :] = tile[1, span, :]
    mine = pl.ds(pl.multiple_of(me * LANES, LANES), LANES)

    def back_copy(off):
        peer = lax.rem(me + off, n)
        return pltpu.make_async_remote_copy(
            src_ref=pk2.at[peer],
            dst_ref=rx2.at[0:8, mine],
            send_sem=back_send.at[off],
            recv_sem=back_recv.at[off],
            device_id=(mp, gx, peer),
            device_id_type=MESH,
        )

    for off in range(1, n):
        back_copy(off).start()
    rx2[0:8, mine] = pk2[me]
    for off in range(1, n):
        back_copy(off).wait_recv()
    rx2[8:16, :] = east_diff(rx2[0:8, :])
    scale = (-0.5 * PUSH_SCALE * levels) / (pk[2 * strip : 3 * strip, :] * total_row)
    for field in range(2):
        force = scale * (
            rx2[8 + field * strip : 8 + (field + 1) * strip, :]
            + rx2[(2 + field) * strip : (3 + field) * strip, :]
        )
        for level in range(levels):
            fields_ref[field, level] = fields_ref[field, level] + share_ref[level] * force

    for off in range(1, n):
        strip_copy(off).wait_send()
        back_copy(off).wait_send()
    drain_pair(depth_copy)
    drain_pair(stress_copy)

    def drain(index, carry):
        drain_edges(lax.div(index, freqs), lax.rem(index, freqs))
        return carry

    lax.fori_loop(0, STEPS * freqs, drain, 0)


def shards(mesh, action, land_mask, bathymetry, surge, ocean_fields, layer_share):
    freqs, dirs, rows, cols = action.shape
    n = mesh.shape["gy"]
    wide = ocean_fields.shape[3]
    f32 = jnp.float32
    dma = pltpu.SemaphoreType.DMA
    vmem = pl.BlockSpec(memory_space=pltpu.VMEM)
    cells = (rows, cols)
    padded = rows + 2 * TOP
    return pl.pallas_call(
        functools.partial(kernel, mesh.shape["mp"], mesh.shape["gx"], n),
        out_shape=(
            jax.ShapeDtypeStruct(action.shape, action.dtype),
            jax.ShapeDtypeStruct(ocean_fields.shape, ocean_fields.dtype),
        ),
        in_specs=[vmem] * 5 + [pl.BlockSpec(memory_space=pltpu.SMEM)],
        out_specs=(vmem, vmem),
        scratch_shapes=[
            pltpu.VMEM((16, wide), f32),
            pltpu.VMEM((n, 8, cols), f32),
            pltpu.VMEM((4,) + cells, f32),
            pltpu.VMEM((padded, cols), f32),
            pltpu.VMEM((2, 8, cols), f32),
            pltpu.VMEM((freqs,) + cells, f32),
            pltpu.VMEM((freqs,) + cells, f32),
            pltpu.VMEM((freqs,) + cells, f32),
            pltpu.VMEM((freqs,) + cells, f32),
            pltpu.VMEM((freqs, dirs // 2) + cells, f32),
            pltpu.VMEM((freqs, dirs, padded, cols), f32),
            pltpu.VMEM((dirs,) + cells, f32),
            pltpu.VMEM((STEPS, freqs) + cells, f32),
            pltpu.VMEM((2, STEPS, freqs) + cells, f32),
            pltpu.VMEM((2, STEPS, freqs, dirs, cols), f32),
            pltpu.VMEM((2, STEPS, freqs, dirs, cols), f32),
            pltpu.VMEM((3,) + cells, f32),
            pltpu.VMEM((2, padded, cols), f32),
            pltpu.VMEM((2, 2, 8, cols), f32),
            pltpu.VMEM((n, 8, cols), f32),
            pltpu.VMEM((16, wide), f32),
            dma((n,)),
            dma((n,)),
            dma((n,)),
            dma((n,)),
            dma((2,)),
            dma((2,)),
            dma((2,)),
            dma((2,)),
            dma((2, STEPS, freqs)),
            dma((2, STEPS, freqs)),
            dma((2, STEPS, freqs)),
            dma((2, STEPS, freqs)),
        ],
        compiler_params=pltpu.CompilerParams(
            collective_id=0, has_side_effects=True, vmem_limit_bytes=40 * 1024 * 1024
        ),
    )(action, land_mask, bathymetry, surge, ocean_fields, layer_share)


def solution(mesh):
    return jax.shard_map(
        functools.partial(shards, mesh),
        mesh=mesh,
        in_specs=(
            P(None, None, ("mp", "gx"), "gy"),
            P(("mp", "gx"), "gy"),
            P(("mp", "gx", "gy"), None),
            P(("mp", "gx", "gy"), None),
            P(None, None, ("mp", "gx", "gy"), None),
            P(),
        ),
        out_specs=(P(None, None, ("mp", "gx"), "gy"), P(None, None, ("mp", "gx", "gy"), None)),
        check_vma=False,
    )
```

```python
import functools
import math

import jax
import jax.numpy as jnp
import numpy as np
from jax import lax
from jax.experimental import pallas as pl
from jax.experimental.pallas import tpu as pltpu
from jax.sharding import PartitionSpec as P

STEPS = 4
GRAVITY = 9.81
STEP_TIME = 14.0
CELL_SIZE = 500.0
FIRST_FREQ = 0.05
FREQ_RATIO = 1.1
MIXING = 0.2
PUSH_SCALE = 20.0
LANES = 128
TOP = 8
MESH = pl.DeviceIdType.MESH


def kernel(
    mesh_mp,
    mesh_gx,
    n,
    action_in,
    land_in,
    bath_in,
    surge_in,
    ocean_in,
    share_ref,
    out_ref,
    fields_ref,
    action_ref,
    land_ref,
    bath_ref,
    surge_ref,
    ocean_ref,
    in_sem,
    pk,
    pk1,
    rx,
    tile,
    dpad,
    dhalo,
    ccg,
    sn,
    hs,
    tb,
    qs,
    xs,
    ps,
    ew_send,
    ew_recv,
    ns_send,
    ns_recv,
    st,
    spad,
    shalo,
    pk2,
    rx2,
    a2a_send,
    a2a_recv,
    back_send,
    back_recv,
    dep_send,
    dep_recv,
    str_send,
    str_recv,
    ew_ssem,
    ew_rsem,
    ns_ssem,
    ns_rsem,
):
    freqs, dirs, rows, cols = action_ref.shape
    levels, strip = ocean_ref.shape[1], ocean_ref.shape[2]
    wide = ocean_ref.shape[3]
    row_count = mesh_mp * mesh_gx
    mp, gx, me = lax.axis_index("mp"), lax.axis_index("gx"), lax.axis_index("gy")
    rank = mp * mesh_gx + gx
    has_south, has_north = rank > 0, rank < row_count - 1
    has_west, has_east = me > 0, me < n - 1
    south_rank = lax.rem(rank + row_count - 1, row_count)
    north_rank = lax.rem(rank + 1, row_count)
    south = (lax.div(south_rank, mesh_gx), lax.rem(south_rank, mesh_gx), me)
    north = (lax.div(north_rank, mesh_gx), lax.rem(north_rank, mesh_gx), me)
    west = (mp, gx, lax.rem(me + n - 1, n))
    east = (mp, gx, lax.rem(me + 1, n))
    angles = np.arange(dirs) * (2.0 * math.pi / dirs)
    cosine = [float(np.float32(v)) for v in np.cos(angles)]
    sine = [float(np.float32(v)) for v in np.sin(angles)]
    courant = STEP_TIME / CELL_SIZE
    turn_scale = STEP_TIME / (2.0 * CELL_SIZE * (2.0 * math.pi / dirs))

    loads = [
        pltpu.make_async_copy(source, target, in_sem.at[index])
        for index, (source, target) in enumerate(
            (
                (ocean_in.at[0:2], ocean_ref.at[0:2]),
                (bath_in, bath_ref),
                (surge_in, surge_ref),
                (action_in, action_ref),
                (ocean_in.at[2:4], ocean_ref.at[2:4]),
                (land_in, land_ref),
            )
        )
    ]
    for load in loads:
        load.start()
    barrier = pltpu.get_barrier_semaphore()
    for off in range(1, n):
        pl.semaphore_signal(
            barrier, inc=1, device_id=(mp, gx, lax.rem(me + off, n)), device_id_type=MESH
        )

    @pl.when(has_south)
    def _():
        pl.semaphore_signal(barrier, inc=1, device_id=south, device_id_type=MESH)

    @pl.when(has_north)
    def _():
        pl.semaphore_signal(barrier, inc=1, device_id=north, device_id_type=MESH)

    for load in loads[:3]:
        load.wait()
    total = share_ref[0]
    for level in range(1, levels):
        total = total + share_ref[level]
    total_row = jnp.full((strip, wide), total, jnp.float32)
    for field in range(2):
        mean = share_ref[0] * ocean_ref[field, 0]
        for level in range(1, levels):
            mean = mean + share_ref[level] * ocean_ref[field, level]
        pk[field * strip : (field + 1) * strip, :] = mean / total_row
    pk[2 * strip : 3 * strip, :] = bath_ref[...] + surge_ref[...]
    wide_lane = lax.broadcasted_iota(jnp.int32, (8, wide), 1)

    def east_diff(value):
        after = jnp.where(wide_lane == wide - 1, 0.0, pltpu.roll(value, wide - 1, 1))
        before = jnp.where(wide_lane == 0, 0.0, pltpu.roll(value, 1, 1))
        return after - before

    pk[8:16, :] = east_diff(pk[0:8, :])
    pk[3 * strip : 4 * strip, :] = pk[8 + 2 * strip : 8 + 3 * strip, :]

    for g in range(n):
        pk1[g] = pk[0:8, g * LANES : (g + 1) * LANES]
    pl.semaphore_wait(barrier, n - 1 + has_south.astype(jnp.int32) + has_north.astype(jnp.int32))

    def strip_copy(off):
        peer = lax.rem(me + off, n)
        return pltpu.make_async_remote_copy(
            src_ref=pk1.at[peer],
            dst_ref=rx.at[me],
            send_sem=a2a_send.at[off],
            recv_sem=a2a_recv.at[off],
            device_id=(mp, gx, peer),
            device_id_type=MESH,
        )

    for off in range(1, n):
        strip_copy(off).start()
    rx[me] = pk1[me]

    def ew_copy(step, freq, side):
        return pltpu.make_async_remote_copy(
            src_ref=ew_send.at[step, freq],
            dst_ref=ew_recv.at[side, step, freq],
            send_sem=ew_ssem.at[side, step, freq],
            recv_sem=ew_rsem.at[side, step, freq],
            device_id=east if side == 0 else west,
            device_id_type=MESH,
        )

    def ns_copy(step, freq, side):
        return pltpu.make_async_remote_copy(
            src_ref=ns_send.at[side, step, freq],
            dst_ref=ns_recv.at[side, step, freq],
            send_sem=ns_ssem.at[side, step, freq],
            recv_sem=ns_rsem.at[side, step, freq],
            device_id=north if side == 0 else south,
            device_id_type=MESH,
        )

    def send_edges(step, freq):
        @pl.when(has_east)
        def _():
            ew_copy(step, freq, 0).start()

        @pl.when(has_west)
        def _():
            ew_copy(step, freq, 1).start()

        @pl.when(has_north)
        def _():
            ns_copy(step, freq, 0).start()

        @pl.when(has_south)
        def _():
            ns_copy(step, freq, 1).start()

    def recv_edges(step, freq):
        @pl.when(has_west)
        def _():
            ew_copy(step, freq, 0).wait_recv()

        @pl.when(has_east)
        def _():
            ew_copy(step, freq, 1).wait_recv()

        @pl.when(has_south)
        def _():
            ns_copy(step, freq, 0).wait_recv()

        @pl.when(has_north)
        def _():
            ns_copy(step, freq, 1).wait_recv()

    def drain_edges(step, freq):
        @pl.when(has_east)
        def _():
            ew_copy(step, freq, 0).wait_send()

        @pl.when(has_west)
        def _():
            ew_copy(step, freq, 1).wait_send()

        @pl.when(has_north)
        def _():
            ns_copy(step, freq, 0).wait_send()

        @pl.when(has_south)
        def _():
            ns_copy(step, freq, 1).wait_send()

    @pl.when(jnp.logical_not(has_west))
    def _():
        ew_recv[0] = jnp.zeros(ew_recv.shape[1:], jnp.float32)

    @pl.when(jnp.logical_not(has_east))
    def _():
        ew_recv[1] = jnp.zeros(ew_recv.shape[1:], jnp.float32)

    @pl.when(jnp.logical_not(has_south))
    def _():
        ns_recv[0] = jnp.zeros(ns_recv.shape[1:], jnp.float32)
        dhalo[0] = jnp.zeros(dhalo.shape[1:], jnp.float32)
        shalo[0] = jnp.zeros(shalo.shape[1:], jnp.float32)

    @pl.when(jnp.logical_not(has_north))
    def _():
        ns_recv[1] = jnp.zeros(ns_recv.shape[1:], jnp.float32)
        dhalo[1] = jnp.zeros(dhalo.shape[1:], jnp.float32)
        shalo[1] = jnp.zeros(shalo.shape[1:], jnp.float32)

    lane = lax.broadcasted_iota(jnp.int32, (rows, cols), 1)
    pair = lane // 2
    even = lane % 2 == 0
    first_lane, last_lane = lane == 0, lane == cols - 1

    def keep(step, freq, d, value, packed):
        xs[freq, d, TOP : TOP + rows, :] = value
        ns_send[0, step, freq, d : d + 1, :] = value[rows - 1 : rows, :]
        ns_send[1, step, freq, d : d + 1, :] = value[0:1, :]
        turned = pltpu.roll(value, 2 * d + 1, 1)
        return jnp.where(pair == d, turned, packed)

    def first_edges(freq, carry):
        packed = jnp.zeros((rows, cols), jnp.float32)
        for d in range(dirs):
            packed = keep(0, freq, d, action_ref[freq, d].astype(jnp.float32), packed)
        ew_send[0, freq] = packed
        send_edges(0, freq)
        return carry

    loads[3].wait()
    lax.fori_loop(0, freqs, first_edges, 0)
    loads[4].wait()
    loads[5].wait()

    for field in range(ocean_ref.shape[0]):
        for level in range(levels):
            here = ocean_ref[field, level]
            upper = ocean_ref[field, max(level - 1, 0)]
            lower = ocean_ref[field, min(level + 1, levels - 1)]
            fields_ref[field, level] = here + MIXING * (upper - 2.0 * here + lower)

    for off in range(1, n):
        strip_copy(off).wait_recv()
    for g in range(n):
        for item in range(4):
            tile[item, g * strip : (g + 1) * strip, :] = rx[g, item * strip : (item + 1) * strip, :]

    def depth_copy(side):
        return pltpu.make_async_remote_copy(
            src_ref=tile.at[2, rows - 8 : rows] if side == 0 else tile.at[2, 0:8],
            dst_ref=dhalo.at[side],
            send_sem=dep_send.at[side],
            recv_sem=dep_recv.at[side],
            device_id=north if side == 0 else south,
            device_id_type=MESH,
        )

    def stress_copy(side):
        return pltpu.make_async_remote_copy(
            src_ref=st.at[1:3, rows - 8 : rows] if side == 0 else st.at[1:3, 0:8],
            dst_ref=shalo.at[side],
            send_sem=str_send.at[side],
            recv_sem=str_recv.at[side],
            device_id=north if side == 0 else south,
            device_id_type=MESH,
        )

    def start_pair(copy):
        @pl.when(has_north)
        def _():
            copy(0).start()

        @pl.when(has_south)
        def _():
            copy(1).start()

    def wait_pair(copy):
        @pl.when(has_south)
        def _():
            copy(0).wait_recv()

        @pl.when(has_north)
        def _():
            copy(1).wait_recv()

    def drain_pair(copy):
        @pl.when(has_north)
        def _():
            copy(0).wait_send()

        @pl.when(has_south)
        def _():
            copy(1).wait_send()

    start_pair(depth_copy)
    depth = tile[2]
    share_of = 1.0 / (freqs * dirs)
    for f in range(freqs):
        sigma = 2.0 * math.pi * FIRST_FREQ * FREQ_RATIO**f
        deep = sigma * sigma / GRAVITY
        number = deep / jnp.sqrt(jnp.tanh(deep * depth))
        twice = 2.0 * number * depth
        grown = jnp.exp(twice)
        inv_sinh = 2.0 / (grown - 1.0 / grown)
        ratio = 0.5 * (1.0 + twice * inv_sinh)
        ccg[f] = (courant * sigma) * ratio / number
        tb[f] = (turn_scale * sigma) * inv_sinh
        sn[f] = (sigma * share_of) * ratio
        hs[f] = jnp.full((rows, cols), 0.5 * sigma * share_of, jnp.float32)
    dpad[TOP : TOP + rows, :] = depth
    wait_pair(depth_copy)
    dpad[TOP - 1 : TOP, :] = dhalo[0, 7:8, :]
    dpad[TOP + rows : TOP + rows + 1, :] = dhalo[1, 0:1, :]
    slope_north = dpad[TOP + 1 : TOP + 1 + rows, :] - dpad[TOP - 1 : TOP - 1 + rows, :]
    slope_east = tile[3]
    for d in range(dirs // 2):
        ps[d] = sine[d] * slope_east - cosine[d] * slope_north

    def turn_rates(freq, carry):
        scale = tb[freq]
        for d in range(dirs // 2):
            raw = scale * ps[d]
            qs[freq, d] = raw / (1.0 + jnp.abs(raw))
        return carry

    lax.fori_loop(0, freqs, turn_rates, 0)
    row = lax.broadcasted_iota(jnp.int32, (rows, cols), 0) + rank * rows
    col = lane + me * cols
    inner = (row > 0) & (row < row_count * rows - 1) & (col > 0) & (col < wide - 1)
    tile[3] = jnp.where(inner, land_ref[...].astype(jnp.float32), 0.0)
    tile[0] = courant * tile[0]
    tile[1] = courant * tile[1]

    def advance(index, carry):
        step, freq = lax.div(index, freqs), lax.rem(index, freqs)
        recv_edges(step, freq)
        merged = jnp.where(
            even,
            pltpu.roll(ew_recv[1, step, freq], cols - 1, 1),
            pltpu.roll(ew_recv[0, step, freq], 1, 1),
        )
        speed = ccg[freq]
        mean_east, mean_north = tile[0], tile[1]
        for d in range(dirs):
            xs[freq, d, TOP - 1 : TOP, :] = ns_recv[0, step, freq, d : d + 1, :]
            xs[freq, d, TOP + rows : TOP + rows + 1, :] = ns_recv[1, step, freq, d : d + 1, :]
        for d in range(dirs):
            value = xs[freq, d, TOP : TOP + rows, :]
            below = xs[freq, d, TOP - 1 : TOP - 1 + rows, :]
            above = xs[freq, d, TOP + 1 : TOP + 1 + rows, :]
            edge = pltpu.roll(merged, cols - 2 * d - 1, 1)
            left = jnp.where(first_lane, edge, pltpu.roll(value, 1, 1))
            right = jnp.where(last_lane, edge, pltpu.roll(value, cols - 1, 1))
            ax = speed * cosine[d] + mean_east
            ay = speed * sine[d] + mean_north
            ps[d] = (
                value
                - jnp.abs(ax) * (value - jnp.where(ax > 0.0, left, right))
                - jnp.abs(ay) * (value - jnp.where(ay > 0.0, below, above))
            )
        wet = tile[3]
        after = lax.rem(step + 1, STEPS)
        packed = jnp.zeros((rows, cols), jnp.float32)
        for d in range(dirs):
            half = d % (dirs // 2)
            rate = qs[freq, half]
            value = ps[d]
            before, following = ps[(d - 1) % dirs], ps[(d + 1) % dirs]
            if d >= dirs // 2:
                before, following = following, before
            turned = value - jnp.abs(rate) * (value - jnp.where(rate > 0.0, before, following))
            rounded = (wet * turned).astype(jnp.bfloat16)
            out_ref[freq, d] = rounded
            value = rounded.astype(jnp.float32)
            xs[freq, d, TOP : TOP + rows, :] = value
            packed = jnp.where(pair == d, pltpu.roll(value, 2 * d + 1, 1), packed)

        @pl.when(step < STEPS - 1)
        def _():
            ew_send[after, freq] = packed
            for d in range(dirs):
                ns_send[0, after, freq, d : d + 1, :] = xs[
                    freq, d, TOP + rows - 1 : TOP + rows, :
                ]
                ns_send[1, after, freq, d : d + 1, :] = xs[freq, d, TOP : TOP + 1, :]
            send_edges(after, freq)

        return carry

    lax.fori_loop(0, STEPS * freqs, advance, 0)

    def stress(freq, carry):
        plain = jnp.zeros((rows, cols), jnp.float32)
        cos_sq, cross = plain, plain
        for d in range(dirs):
            value = xs[freq, d, TOP : TOP + rows, :]
            plain = plain + value
            cos_sq = cos_sq + (cosine[d] * cosine[d]) * value
            cross = cross + (cosine[d] * sine[d]) * value
        scaled, half = sn[freq], hs[freq] * plain
        return (
            carry[0] + scaled * (cos_sq + plain) - half,
            carry[1] + scaled * cross,
            carry[2] + scaled * (2.0 * plain - cos_sq) - half,
        )

    zero = jnp.zeros((rows, cols), jnp.float32)
    sums = lax.fori_loop(0, freqs, stress, (zero, zero, zero))
    for item in range(3):
        st[item] = sums[item]
    start_pair(stress_copy)
    for item in range(2):
        spad[item, TOP : TOP + rows, :] = sums[1 + item]
    wait_pair(stress_copy)
    for item in range(2):
        spad[item, TOP - 1 : TOP, :] = shalo[0, item, 7:8, :]
        spad[item, TOP + rows : TOP + rows + 1, :] = shalo[1, item, 0:1, :]
    for item in range(2):
        tile[item] = (
            spad[item, TOP + 1 : TOP + 1 + rows, :] - spad[item, TOP - 1 : TOP - 1 + rows, :]
        )
    for g in range(n):
        span = slice(g * strip, (g + 1) * strip)
        pk2[g, 0:strip, :] = st[0, span, :]
        pk2[g, strip : 2 * strip, :] = st[1, span, :]
        pk2[g, 2 * strip : 3 * strip, :] = tile[0, span, :]
        pk2[g, 3 * strip : 4 * strip, :] = tile[1, span, :]
    mine = pl.ds(pl.multiple_of(me * LANES, LANES), LANES)

    def back_copy(off):
        peer = lax.rem(me + off, n)
        return pltpu.make_async_remote_copy(
            src_ref=pk2.at[peer],
            dst_ref=rx2.at[0:8, mine],
            send_sem=back_send.at[off],
            recv_sem=back_recv.at[off],
            device_id=(mp, gx, peer),
            device_id_type=MESH,
        )

    for off in range(1, n):
        back_copy(off).start()
    rx2[0:8, mine] = pk2[me]
    for off in range(1, n):
        back_copy(off).wait_recv()
    rx2[8:16, :] = east_diff(rx2[0:8, :])
    scale = (-0.5 * PUSH_SCALE * levels) / (pk[2 * strip : 3 * strip, :] * total_row)
    for field in range(2):
        force = scale * (
            rx2[8 + field * strip : 8 + (field + 1) * strip, :]
            + rx2[(2 + field) * strip : (3 + field) * strip, :]
        )
        for level in range(levels):
            fields_ref[field, level] = fields_ref[field, level] + share_ref[level] * force

    for off in range(1, n):
        strip_copy(off).wait_send()
        back_copy(off).wait_send()
    drain_pair(depth_copy)
    drain_pair(stress_copy)

    def drain(index, carry):
        drain_edges(lax.div(index, freqs), lax.rem(index, freqs))
        return carry

    lax.fori_loop(0, STEPS * freqs, drain, 0)


def shards(mesh, action, land_mask, bathymetry, surge, ocean_fields, layer_share):
    freqs, dirs, rows, cols = action.shape
    n = mesh.shape["gy"]
    wide = ocean_fields.shape[3]
    f32 = jnp.float32
    dma = pltpu.SemaphoreType.DMA
    vmem = pl.BlockSpec(memory_space=pltpu.VMEM)
    cells = (rows, cols)
    padded = rows + 2 * TOP
    return pl.pallas_call(
        functools.partial(kernel, mesh.shape["mp"], mesh.shape["gx"], n),
        out_shape=(
            jax.ShapeDtypeStruct(action.shape, action.dtype),
            jax.ShapeDtypeStruct(ocean_fields.shape, ocean_fields.dtype),
        ),
        in_specs=[pl.BlockSpec(memory_space=pltpu.HBM)] * 5 + [pl.BlockSpec(memory_space=pltpu.SMEM)],
        out_specs=(vmem, vmem),
        scratch_shapes=[
            pltpu.VMEM(action.shape, action.dtype),
            pltpu.VMEM(land_mask.shape, land_mask.dtype),
            pltpu.VMEM(bathymetry.shape, f32),
            pltpu.VMEM(surge.shape, f32),
            pltpu.VMEM(ocean_fields.shape, f32),
            dma((6,)),
            pltpu.VMEM((16, wide), f32),
            pltpu.VMEM((n, 8, cols), f32),
            pltpu.VMEM((n, 8, cols), f32),
            pltpu.VMEM((4,) + cells, f32),
            pltpu.VMEM((padded, cols), f32),
            pltpu.VMEM((2, 8, cols), f32),
            pltpu.VMEM((freqs,) + cells, f32),
            pltpu.VMEM((freqs,) + cells, f32),
            pltpu.VMEM((freqs,) + cells, f32),
            pltpu.VMEM((freqs,) + cells, f32),
            pltpu.VMEM((freqs, dirs // 2) + cells, f32),
            pltpu.VMEM((freqs, dirs, padded, cols), f32),
            pltpu.VMEM((dirs,) + cells, f32),
            pltpu.VMEM((STEPS, freqs) + cells, f32),
            pltpu.VMEM((2, STEPS, freqs) + cells, f32),
            pltpu.VMEM((2, STEPS, freqs, dirs, cols), f32),
            pltpu.VMEM((2, STEPS, freqs, dirs, cols), f32),
            pltpu.VMEM((3,) + cells, f32),
            pltpu.VMEM((2, padded, cols), f32),
            pltpu.VMEM((2, 2, 8, cols), f32),
            pltpu.VMEM((n, 8, cols), f32),
            pltpu.VMEM((16, wide), f32),
            dma((n,)),
            dma((n,)),
            dma((n,)),
            dma((n,)),
            dma((2,)),
            dma((2,)),
            dma((2,)),
            dma((2,)),
            dma((2, STEPS, freqs)),
            dma((2, STEPS, freqs)),
            dma((2, STEPS, freqs)),
            dma((2, STEPS, freqs)),
        ],
        compiler_params=pltpu.CompilerParams(
            collective_id=0, has_side_effects=True, vmem_limit_bytes=60 * 1024 * 1024
        ),
    )(action, land_mask, bathymetry, surge, ocean_fields, layer_share)


def solution(mesh):
    return jax.shard_map(
        functools.partial(shards, mesh),
        mesh=mesh,
        in_specs=(
            P(None, None, ("mp", "gx"), "gy"),
            P(("mp", "gx"), "gy"),
            P(("mp", "gx", "gy"), None),
            P(("mp", "gx", "gy"), None),
            P(None, None, ("mp", "gx", "gy"), None),
            P(),
        ),
        out_specs=(P(None, None, ("mp", "gx"), "gy"), P(None, None, ("mp", "gx", "gy"), None)),
        check_vma=False,
    )
```
